32 devices in a mesh: tensor: 2 (over x), expert: 16 (over z, y, core).
Axes of the slice: x: 2, y: 2, z: 4, core: 2. Of those that a mesh axis runs over, the one named last changes fastest.
Arguments:
- out_grad: bfloat16 [16, 32, 4096], P('expert', 'tensor'), may hold values from -6 to 6
- norm_input: bfloat16 [16, 32, 4096], P('expert', 'tensor'), may hold values from -24 to 24
- norm_gain: float32 [4096], replicated, may hold values from 0.3 to 3
- routes: int32 [16, 32, 8], P('expert'), may hold values from 0 to 15, all different within a row; in each aligned block of 32 rows (0 to 31, 32 to 63, ..., all dimensions but the last counted through in order) at most 32 rows name the same one
- route_weight: float32 [16, 32, 8], P('expert'), may hold values from 0.05 to 0.25
- gate_saved: bfloat16 [16, 512, 1024], P('expert', None, 'tensor'), may hold values from -8 to 8
- up_saved: bfloat16 [16, 512, 1024], P('expert', None, 'tensor'), may hold values from -6 to 6
- w_gate: bfloat16 [16, 4096, 1024], P('expert', None, 'tensor'), may hold values from -0.09375 to 0.09375
- w_up: bfloat16 [16, 4096, 1024], P('expert', None, 'tensor'), may hold values from -0.09375 to 0.09375
- w_down: bfloat16 [16, 1024, 4096], P('expert', 'tensor'), may hold values from -0.1875 to 0.1875
- out_proj: bfloat16 [4096, 4096], P('tensor', 'expert'), may hold values from -0.09375 to 0.09375
Outputs:
- resid_grad: bfloat16 [16, 32, 4096], P('expert', 'tensor')
- attn_grad: bfloat16 [16, 32, 4096], P('expert', None, 'tensor')
- down_grad: bfloat16 [16, 1024, 4096], P('expert', 'tensor')
The draws below stay inside these ranges and needn't reach their ends.
Inputs may be any that keep to these rules, and one draw needn't show every extreme that they name: Each token names 8 different experts. Among the tokens of one group no expert is named by more than 32 routes, and in some group some expert is named by exactly 32.
All inputs are finite; a program needn't handle non-finite values.
Results may differ from the reference program's by a relative error of at most 0.015.
Values may be sent and summed in bfloat16 or wider, within the bound.
A program may use at most 128 MiB of HBM per device.

```python
import math
import jax
import jax.numpy as jnp
import numpy as np
from jax import lax

D = 4096
HID = 1024
QDIM = 4096
TOP = 8
TOK_GRP = 32
EXPERTS = 16
GROUPS = 16
CAP = 32
SLOTS = 512
N_TENSOR = 2


def draw_norm_input(key, part):
    key_base, key_rows, key_cols = jax.random.split(key, 3)
    values = jax.random.normal(key_base, (GROUPS, TOK_GRP, D), jnp.float32)
    row_low = math.log(0.3)
    row_high = math.log(3.0)
    row_scale = jnp.exp(jax.random.uniform(key_rows, (GROUPS, TOK_GRP, 1), jnp.float32, row_low, row_high))
    col_scale = jnp.exp(jax.random.uniform(key_cols, (1, 1, D), jnp.float32, math.log(0.3), math.log(3.0)))
    return jnp.clip(values * row_scale * col_scale, -24.0, 24.0).astype(jnp.bfloat16)


def block_scale(key, dims, pieces, smallest, high):
    factor_of, own = 1.0, jax.random.fold_in(key, 6)
    for axis_at, shards_of in pieces:
        steps = jnp.exp(jax.random.uniform(jax.random.fold_in(own, axis_at), (shards_of,), jnp.float32, smallest / len(pieces), high / len(pieces)))
        factor_of = factor_of * jnp.repeat(steps, dims[axis_at] // shards_of).reshape([-1 if axis == axis_at else 1 for axis in range(len(dims))])
    return factor_of


def assign_block(rng, own, number, rows, number_of, top, bound, slope):
    ranking = jax.random.permutation(rng, number_of)
    crowded, usual = load_shares(number_of, rows * top, bound, slope, True), load_shares(number_of, rows * top, bound, slope, False)
    places = jnp.arange(number_of)

    def named(sizes, offset_by):
        used = int((sizes > 0).sum())
        fixed = max(1, used // 4)
        shifted = fixed + (places - fixed + offset_by * (used - fixed)) % max(1, number_of - fixed)
        return jnp.zeros((number_of,), jnp.int32).at[ranking[jnp.where(places < fixed, places, shifted)]].set(jnp.asarray(sizes, jnp.int32))

    sizes = jnp.where(number % 4 == 0, named(crowded, number // 4), named(usual, number - number // 4 - 1))
    mixed = jax.random.permutation(jax.random.fold_in(own, 3), number_of)
    source_of, sink = mixed[0:number_of // 2 * 2:2], mixed[1:number_of // 2 * 2:2]
    margin = jnp.minimum(sizes[source_of] - 1, bound - sizes[sink]) // 2
    margin = jnp.where((source_of == ranking[0]) | (sink == ranking[0]) | (sizes[sink] == 0), 0, jnp.maximum(margin, 0))
    shifted = jax.random.randint(jax.random.fold_in(own, 4), (number_of // 2,), 0, 1 << 20) % (margin + 1)
    sizes = sizes.at[source_of].add(-shifted).at[sink].add(shifted)
    members = jnp.searchsorted(jnp.cumsum(sizes), jnp.arange(rows * top), side="right").astype(jnp.int32)
    grid = members.reshape(top, rows).T
    grid = grid[jax.random.permutation(jax.random.fold_in(own, 1), rows)]
    offset_by = jax.random.randint(jax.random.fold_in(own, 2), (rows, 1), 0, top)
    return jnp.take_along_axis(grid, (jnp.arange(top)[None, :] + offset_by) % top, axis=1)


def load_shares(number_of, total, bound, skew, full):
    portions = [(1 << 20) // math.isqrt(standing ** skew) + 1 for standing in range(1, number_of + 1)]
    largest = bound if full else min(bound, max(-(-total // number_of), total * portions[0] // sum(portions)))
    least = 1 if total - largest >= number_of - 1 else 0
    holding, rest = [largest] + [least] * (number_of - 1), total - largest - least * (number_of - 1)
    while rest > 0:
        candidates = [i for i in range(1, number_of) if holding[i] < largest] or [i for i in range(1, number_of) if holding[i] < bound]
        mass, budget = sum([portions[i] for i in candidates]), rest
        for i in candidates:
            extra = min(bound - holding[i], max(1, budget * portions[i] // mass), rest)
            holding[i] = holding[i] + extra
            rest = rest - extra
    return np.array(holding)


def gaussian(key, shape, scale, most, cuts=(), held_as=jnp.bfloat16):
    factor_of = block_scale(key, shape, cuts, -0.22, 0.18) if cuts else 1.0
    drawn = jax.random.normal(key, shape, jnp.float32) * scale * factor_of
    return jnp.minimum(jnp.maximum(drawn, -most), most).astype(held_as)


def setup_inputs(seed: int = 0) -> dict:
    arg_keys = jax.random.split(jax.random.key(seed), 12)
    out_grad = gaussian(arg_keys[0], (GROUPS, TOK_GRP, D), 1.0, 6.0, ((0, 16), (1, 2)))
    norm_input = draw_norm_input(jax.random.fold_in(arg_keys[11], 71), 0)
    norm_gain = jnp.clip(jnp.exp(jax.random.uniform(arg_keys[2], (D,), jnp.float32, math.log(0.3), math.log(3.0))), 0.3, 3.0)
    routes_keys = jax.random.split(jax.random.fold_in(arg_keys[3], 1), GROUPS * TOK_GRP // TOK_GRP)
    routes_turns = jax.random.permutation(jax.random.fold_in(arg_keys[3], 3), GROUPS * TOK_GRP // TOK_GRP)
    routes = jax.vmap(lambda own, number: assign_block(jax.random.fold_in(arg_keys[3], 2), own, number, TOK_GRP, EXPERTS, TOP, CAP, 2))(routes_keys, routes_turns).reshape((GROUPS, TOK_GRP, TOP))
    route_weight = jnp.clip(0.05 + 0.2 * jax.random.uniform(arg_keys[4], (GROUPS, TOK_GRP, TOP), jnp.float32) ** block_scale(arg_keys[4], (GROUPS, TOK_GRP, TOP), ((0, 16),), -0.2, 0.2), 0.05, 0.25)
    gate_saved = gaussian(arg_keys[5], (EXPERTS, SLOTS, HID), 1.5, 8.0, ((0, 16), (2, 2)))
    up_saved = gaussian(arg_keys[6], (EXPERTS, SLOTS, HID), 1.0, 6.0, ((0, 16), (2, 2)))
    w_gate = gaussian(arg_keys[7], (EXPERTS, D, HID), D ** -0.5, 0.09375, ((0, 16), (2, 2)))
    w_up = gaussian(arg_keys[8], (EXPERTS, D, HID), D ** -0.5, 0.09375, ((0, 16), (2, 2)))
    w_down = gaussian(arg_keys[9], (EXPERTS, HID, D), HID ** -0.5, 0.1875, ((0, 16), (1, 2)))
    out_proj = gaussian(arg_keys[10], (QDIM, D), QDIM ** -0.5, 0.09375, ((0, 2), (1, 16)))
    return {"out_grad": out_grad, "norm_input": norm_input, "norm_gain": norm_gain, "routes": routes, "route_weight": route_weight, "gate_saved": gate_saved, "up_saved": up_saved, "w_gate": w_gate, "w_up": w_up, "w_down": w_down, "out_proj": out_proj}


def slot_ranks(routes):
    route_ids = routes.reshape(GROUPS, TOK_GRP * TOP)
    one_hot = (route_ids[:, :, None] == jnp.arange(EXPERTS, dtype=jnp.int32)[None, None, :]).astype(jnp.int32)
    earlier = jnp.cumsum(one_hot, axis=1) - one_hot
    slot_rank = lax.optimization_barrier(jnp.sum(earlier * one_hot, axis=2)).astype(jnp.int32)
    return (route_ids, slot_rank)

def reference(out_grad, norm_input, norm_gain, routes, route_weight, gate_saved, up_saved, w_gate, w_up, w_down, out_proj):
    route_total = TOK_GRP * TOP
    route_ids, slot_rank = slot_ranks(routes)
    position = route_ids * CAP + slot_rank
    group_index = jnp.arange(GROUPS, dtype=jnp.int32)[:, None]
    route_index = jnp.broadcast_to(jnp.arange(route_total, dtype=jnp.int32)[None, :], (GROUPS, route_total))
    source = jnp.full((GROUPS, EXPERTS * CAP), -1, jnp.int32).at[group_index, position].set(route_index)
    filled = source >= 0
    safe_source = jnp.where(filled, source, 0).astype(jnp.int32)
    weight_flat = route_weight.reshape(GROUPS, route_total)
    slot_weight = jnp.where(filled, jnp.take_along_axis(weight_flat, safe_source, axis=1), jnp.float32(0.0))
    slot_token = (safe_source // TOP).astype(jnp.int32)
    block_width = HID // N_TENSOR

    def per_expert(expert_id):
        start = (expert_id * CAP).astype(jnp.int32)
        token_ids = lax.dynamic_slice_in_dim(slot_token, start, CAP, 1)
        weights = lax.dynamic_slice_in_dim(slot_weight, start, CAP, 1)
        picked_rows = out_grad[group_index, token_ids]
        slot_grad = (weights[:, :, None] * picked_rows.astype(jnp.float32)).astype(jnp.bfloat16)
        slot_grad = slot_grad.reshape(GROUPS * CAP, D)
        gate = gate_saved[expert_id].astype(jnp.float32)
        upper = up_saved[expert_id].astype(jnp.float32)
        hid_grad = jnp.dot(slot_grad, w_down[expert_id].T, preferred_element_type=jnp.float32)
        sigmoid_gate = jax.nn.sigmoid(gate)
        activation = gate * sigmoid_gate
        gate_grad = (hid_grad * upper * sigmoid_gate * (1.0 + gate * (1.0 - sigmoid_gate))).astype(jnp.bfloat16)
        up_grad = (hid_grad * activation).astype(jnp.bfloat16)
        hidden = (activation * upper).astype(jnp.bfloat16)
        gate_blocks = gate_grad.astype(jnp.float32).reshape(GROUPS * CAP, N_TENSOR, block_width)
        up_blocks = up_grad.astype(jnp.float32).reshape(GROUPS * CAP, N_TENSOR, block_width)
        gate_weights = w_gate[expert_id].astype(jnp.float32).reshape(D, N_TENSOR, block_width)
        up_weights = w_up[expert_id].astype(jnp.float32).reshape(D, N_TENSOR, block_width)
        part_grad = jnp.einsum('jbh,dbh->bjd', gate_blocks, gate_weights) + jnp.einsum('jbh,dbh->bjd', up_blocks, up_weights)
        part_grad = part_grad.astype(jnp.bfloat16)
        slot_sum = lax.optimization_barrier(jnp.sum(part_grad.astype(jnp.float32), axis=0))
        down_grad = jnp.dot(hidden.T, slot_grad, preferred_element_type=jnp.float32).astype(jnp.bfloat16)
        return (slot_sum, down_grad)
    slot_sums, down_grad = lax.map(per_expert, jnp.arange(EXPERTS, dtype=jnp.int32))
    picked = slot_sums[route_ids, group_index * CAP + slot_rank]
    moe_grad = lax.optimization_barrier(jnp.sum(picked.reshape(GROUPS, TOK_GRP, TOP, D), axis=2))
    resid_in = norm_input.astype(jnp.float32)
    inv_rms = lax.rsqrt(lax.optimization_barrier(jnp.mean(resid_in * resid_in, axis=-1, keepdims=True)) + 1e-06)
    scaled_grad = norm_gain * moe_grad
    projection = lax.optimization_barrier(jnp.sum(scaled_grad * resid_in, axis=-1, keepdims=True))
    resid_grad = out_grad.astype(jnp.float32) + inv_rms * scaled_grad - inv_rms * inv_rms * inv_rms / D * resid_in * projection
    resid_grad = resid_grad.astype(jnp.bfloat16)
    attn_grad = jnp.dot(resid_grad.reshape(GROUPS * TOK_GRP, D), out_proj.T, preferred_element_type=jnp.float32)
    attn_grad = attn_grad.astype(jnp.bfloat16).reshape(GROUPS, TOK_GRP, QDIM)
    return (resid_grad, attn_grad, down_grad)
```

```python
import jax
import jax.numpy as jnp
from jax import lax
from jax.sharding import PartitionSpec as P


def slot_position(route_ids, slot_cap, expert_count):
    flat_ids = route_ids.reshape(-1)
    one_hot = (flat_ids[:, None] == jnp.arange(expert_count, dtype=jnp.int32)[None, :]).astype(
        jnp.int32
    )
    earlier = jnp.cumsum(one_hot, axis=0) - one_hot
    slot_rank = jnp.sum(earlier * one_hot, axis=1)
    return flat_ids * slot_cap + slot_rank


def weighted_rows(token_rows, slot_token, slot_weight):
    picked_rows = token_rows[slot_token]
    return (slot_weight[:, None] * picked_rows.astype(jnp.float32)).astype(jnp.bfloat16)


def per_device_slots(
    out_grad,
    norm_input,
    norm_gain,
    routes,
    route_weight,
    gate_saved,
    up_saved,
    w_gate,
    w_up,
    w_down,
    out_proj,
):
    expert_count = lax.axis_size("expert")
    slot_cap = gate_saved.shape[1] // expert_count
    top_count = routes.shape[2]
    route_total = routes.shape[1] * top_count
    model_width = out_grad.shape[2]
    position = slot_position(routes[0], slot_cap, expert_count)
    source = (
        jnp.full((expert_count * slot_cap,), -1, jnp.int32)
        .at[position]
        .set(jnp.arange(route_total, dtype=jnp.int32))
    )
    filled = source >= 0
    safe_source = jnp.where(filled, source, 0)
    slot_weight = jnp.where(filled, route_weight[0].reshape(-1)[safe_source], jnp.float32(0.0))
    slot_token = safe_source // top_count
    group_grads = lax.all_gather(out_grad, "tensor", axis=1, tiled=True)
    scaled = weighted_rows(group_grads[0], slot_token, slot_weight)
    received = lax.all_to_all(
        scaled.reshape(expert_count, slot_cap, model_width),
        "expert",
        split_axis=0,
        concat_axis=0,
        tiled=True,
    )
    slot_grad = received.reshape(expert_count * slot_cap, model_width)
    contract_last = (((1,), (1,)), ((), ()))
    hid_grad = lax.dot_general(
        slot_grad, w_down[0], contract_last, preferred_element_type=jnp.float32
    )
    gate = gate_saved[0].astype(jnp.float32)
    upper = up_saved[0].astype(jnp.float32)
    sigmoid_gate = jax.nn.sigmoid(gate)
    activation = gate * sigmoid_gate
    gate_grad = (hid_grad * upper * sigmoid_gate * (1.0 + gate * (1.0 - sigmoid_gate))).astype(
        jnp.bfloat16
    )
    up_grad = (hid_grad * activation).astype(jnp.bfloat16)
    part_grad = lax.dot_general(
        gate_grad, w_gate[0], contract_last, preferred_element_type=jnp.float32
    )
    part_grad = part_grad + lax.dot_general(
        up_grad, w_up[0], contract_last, preferred_element_type=jnp.float32
    )
    part_grad = part_grad.astype(jnp.bfloat16)
    hidden = (activation * upper).astype(jnp.bfloat16)
    contract_first = (((0,), (0,)), ((), ()))
    block_sums = lax.psum_scatter(
        part_grad.astype(jnp.float32).astype(jnp.bfloat16),
        "tensor",
        scatter_dimension=1,
        tiled=True,
    ).astype(jnp.float32)
    feature_width = block_sums.shape[1]
    came_back = lax.all_to_all(
        block_sums.reshape(expert_count, slot_cap, feature_width).astype(jnp.bfloat16),
        "expert",
        split_axis=0,
        concat_axis=0,
        tiled=True,
    ).astype(jnp.float32)
    picked_part = came_back.reshape(expert_count * slot_cap, feature_width)[position]
    part_sum = jnp.sum(picked_part.reshape(-1, top_count, feature_width), axis=1)
    moe_grad = lax.all_to_all(
        part_sum.astype(jnp.bfloat16), "tensor", split_axis=0, concat_axis=1, tiled=True
    ).astype(part_sum.dtype)
    down_grad = lax.dot_general(
        hidden, slot_grad, contract_first, preferred_element_type=jnp.float32
    )
    down_grad = down_grad.astype(jnp.bfloat16)[None]
    resid_in = norm_input[0].astype(jnp.float32)
    inv_rms = lax.rsqrt(jnp.mean(resid_in * resid_in, axis=-1, keepdims=True) + 1e-06)
    scaled_grad = norm_gain * moe_grad
    projection = jnp.sum(scaled_grad * resid_in, axis=-1, keepdims=True)
    resid_grad = (
        out_grad[0].astype(jnp.float32)
        + inv_rms * scaled_grad
        - inv_rms * inv_rms * inv_rms / model_width * resid_in * projection
    )
    resid_grad = resid_grad.astype(jnp.bfloat16)[None]
    group_resid = lax.all_gather(resid_grad, "tensor", axis=1, tiled=True)
    group_rows = group_resid[0]
    attn_sum = lax.dot_general(
        group_rows,
        lax.all_gather(out_proj, "expert", axis=1, tiled=True),
        contract_last,
        preferred_element_type=jnp.float32,
    )
    attn_grad = attn_sum.astype(jnp.bfloat16)[None]
    return (resid_grad, attn_grad, down_grad)


def per_device_tokens(
    out_grad,
    norm_input,
    norm_gain,
    routes,
    route_weight,
    gate_saved,
    up_saved,
    w_gate,
    w_up,
    w_down,
    out_proj,
):
    everyone = ("expert", "tensor")
    expert_count = lax.axis_size("expert")
    expert = lax.axis_index("expert")
    slot_total = gate_saved.shape[1]
    slot_cap = slot_total // expert_count
    group_tokens = routes.shape[1]
    model_width = out_grad.shape[2]
    token_total = expert_count * group_tokens
    contract_last = (((1,), (1,)), ((), ()))
    contract_first = (((0,), (0,)), ((), ()))

    dense = jnp.sum(
        jnp.where(
            routes[0][:, :, None] == jnp.arange(expert_count, dtype=jnp.int32)[None, None, :],
            route_weight[0][:, :, None],
            0.0,
        ),
        axis=1,
    )
    all_dense = lax.all_gather(dense, "expert", axis=0, tiled=False)
    weight = lax.dynamic_index_in_dim(all_dense, expert, axis=2, keepdims=False)
    named = weight > 0.0
    before = jnp.tril(jnp.ones((group_tokens, group_tokens), jnp.float32), -1)
    rank = jnp.einsum("gt,ut->gu", named.astype(jnp.float32), before).astype(jnp.int32)
    slot = jnp.arange(expert_count, dtype=jnp.int32)[:, None] * slot_cap + rank
    slot = jnp.where(named, slot, -1).reshape(token_total, 1)
    pick = (slot == jnp.arange(slot_total, dtype=jnp.int32)[None, :]).astype(jnp.bfloat16)
    gate = lax.dot_general(
        pick, gate_saved[0], (((1,), (0,)), ((), ())), preferred_element_type=jnp.float32
    )
    upper = lax.dot_general(
        pick, up_saved[0], (((1,), (0,)), ((), ())), preferred_element_type=jnp.float32
    )
    sigmoid_gate = jax.nn.sigmoid(gate)
    activation = gate * sigmoid_gate
    hidden = (activation * upper).astype(jnp.bfloat16)

    all_grads = lax.all_gather(out_grad[0], everyone, axis=0, tiled=True)
    token_grad = (weight.reshape(token_total, 1) * all_grads.astype(jnp.float32)).astype(
        jnp.bfloat16
    )
    hid_grad = lax.dot_general(
        token_grad, w_down[0], contract_last, preferred_element_type=jnp.float32
    )
    gate_grad = (hid_grad * upper * sigmoid_gate * (1.0 + gate * (1.0 - sigmoid_gate))).astype(
        jnp.bfloat16
    )
    up_grad = (hid_grad * activation).astype(jnp.bfloat16)
    part_grad = lax.dot_general(
        gate_grad, w_gate[0], contract_last, preferred_element_type=jnp.float32
    )
    part_grad = part_grad + lax.dot_general(
        up_grad, w_up[0], contract_last, preferred_element_type=jnp.float32
    )
    part_grad = part_grad.astype(jnp.bfloat16)
    moe_grad = lax.psum_scatter(
        part_grad, everyone, scatter_dimension=0, tiled=True
    ).astype(jnp.float32)
    down_grad = lax.dot_general(
        hidden, token_grad, contract_first, preferred_element_type=jnp.float32
    )
    down_grad = down_grad.astype(jnp.bfloat16)[None]
    resid_in = norm_input[0].astype(jnp.float32)
    inv_rms = lax.rsqrt(jnp.mean(resid_in * resid_in, axis=-1, keepdims=True) + 1e-06)
    scaled_grad = norm_gain * moe_grad
    projection = jnp.sum(scaled_grad * resid_in, axis=-1, keepdims=True)
    resid_grad = (
        out_grad[0].astype(jnp.float32)
        + inv_rms * scaled_grad
        - inv_rms * inv_rms * inv_rms / model_width * resid_in * projection
    )
    resid_grad = resid_grad.astype(jnp.bfloat16)
    own_rows = resid_grad.shape[0]
    columns = lax.all_to_all(
        resid_grad.reshape(own_rows, expert_count, -1),
        "expert",
        split_axis=1,
        concat_axis=0,
        tiled=True,
    ).reshape(expert_count, own_rows, -1)
    columns = lax.all_gather(columns, "tensor", axis=1, tiled=True).reshape(token_total, -1)
    attn_part = lax.dot_general(
        columns, out_proj, contract_last, preferred_element_type=jnp.float32
    ).astype(jnp.bfloat16)
    attn_grad = lax.psum_scatter(attn_part, "expert", scatter_dimension=0, tiled=True)
    return (resid_grad[None], attn_grad[None], down_grad)


def per_device(*args):
    token_total = lax.axis_size("expert") * args[3].shape[1]
    if token_total <= args[5].shape[1]:
        return per_device_tokens(*args)
    return per_device_slots(*args)


def solution(mesh):
    placed = (
        P("expert", "tensor", None),
        P("expert", "tensor", None),
        P(),
        P("expert", None, None),
        P("expert", None, None),
        P("expert", None, "tensor"),
        P("expert", None, "tensor"),
        P("expert", None, "tensor"),
        P("expert", None, "tensor"),
        P("expert", "tensor", None),
        P("tensor", "expert"),
    )
    return jax.shard_map(
        per_device,
        mesh=mesh,
        in_specs=placed,
        out_specs=(
            P("expert", "tensor", None),
            P("expert", None, "tensor"),
            P("expert", "tensor", None),
        ),
        check_vma=False,
    )
```

```python
import functools
import jax
import jax.numpy as jnp
from jax import lax
from jax.experimental import pallas as pl
from jax.experimental.pallas import tpu as pltpu
from jax.sharding import PartitionSpec as P


def slot_position(route_ids, slot_cap, expert_count):
    flat_ids = route_ids.reshape(-1)
    one_hot = (flat_ids[:, None] == jnp.arange(expert_count, dtype=jnp.int32)[None, :]).astype(
        jnp.int32
    )
    earlier = jnp.cumsum(one_hot, axis=0) - one_hot
    slot_rank = jnp.sum(earlier * one_hot, axis=1)
    return flat_ids * slot_cap + slot_rank


def weighted_rows(token_rows, slot_token, slot_weight):
    picked_rows = token_rows[slot_token]
    return (slot_weight[:, None] * picked_rows.astype(jnp.float32)).astype(jnp.bfloat16)


def per_device_slots(
    out_grad,
    norm_input,
    norm_gain,
    routes,
    route_weight,
    gate_saved,
    up_saved,
    w_gate,
    w_up,
    w_down,
    out_proj,
):
    expert_count = lax.axis_size("expert")
    slot_cap = gate_saved.shape[1] // expert_count
    top_count = routes.shape[2]
    route_total = routes.shape[1] * top_count
    model_width = out_grad.shape[2]
    position = slot_position(routes[0], slot_cap, expert_count)
    source = (
        jnp.full((expert_count * slot_cap,), -1, jnp.int32)
        .at[position]
        .set(jnp.arange(route_total, dtype=jnp.int32))
    )
    filled = source >= 0
    safe_source = jnp.where(filled, source, 0)
    slot_weight = jnp.where(filled, route_weight[0].reshape(-1)[safe_source], jnp.float32(0.0))
    slot_token = safe_source // top_count
    group_grads = lax.all_gather(out_grad, "tensor", axis=1, tiled=True)
    scaled = weighted_rows(group_grads[0], slot_token, slot_weight)
    received = lax.all_to_all(
        scaled.reshape(expert_count, slot_cap, model_width),
        "expert",
        split_axis=0,
        concat_axis=0,
        tiled=True,
    )
    slot_grad = received.reshape(expert_count * slot_cap, model_width)
    contract_last = (((1,), (1,)), ((), ()))
    hid_grad = lax.dot_general(
        slot_grad, w_down[0], contract_last, preferred_element_type=jnp.float32
    )
    gate = gate_saved[0].astype(jnp.float32)
    upper = up_saved[0].astype(jnp.float32)
    sigmoid_gate = jax.nn.sigmoid(gate)
    activation = gate * sigmoid_gate
    gate_grad = (hid_grad * upper * sigmoid_gate * (1.0 + gate * (1.0 - sigmoid_gate))).astype(
        jnp.bfloat16
    )
    up_grad = (hid_grad * activation).astype(jnp.bfloat16)
    part_grad = lax.dot_general(
        gate_grad, w_gate[0], contract_last, preferred_element_type=jnp.float32
    )
    part_grad = part_grad + lax.dot_general(
        up_grad, w_up[0], contract_last, preferred_element_type=jnp.float32
    )
    part_grad = part_grad.astype(jnp.bfloat16)
    hidden = (activation * upper).astype(jnp.bfloat16)
    contract_first = (((0,), (0,)), ((), ()))
    block_sums = lax.psum_scatter(
        part_grad.astype(jnp.float32).astype(jnp.bfloat16),
        "tensor",
        scatter_dimension=1,
        tiled=True,
    ).astype(jnp.float32)
    feature_width = block_sums.shape[1]
    came_back = lax.all_to_all(
        block_sums.reshape(expert_count, slot_cap, feature_width).astype(jnp.bfloat16),
        "expert",
        split_axis=0,
        concat_axis=0,
        tiled=True,
    ).astype(jnp.float32)
    picked_part = came_back.reshape(expert_count * slot_cap, feature_width)[position]
    part_sum = jnp.sum(picked_part.reshape(-1, top_count, feature_width), axis=1)
    moe_grad = lax.all_to_all(
        part_sum.astype(jnp.bfloat16), "tensor", split_axis=0, concat_axis=1, tiled=True
    ).astype(part_sum.dtype)
    down_grad = lax.dot_general(
        hidden, slot_grad, contract_first, preferred_element_type=jnp.float32
    )
    down_grad = down_grad.astype(jnp.bfloat16)[None]
    resid_in = norm_input[0].astype(jnp.float32)
    inv_rms = lax.rsqrt(jnp.mean(resid_in * resid_in, axis=-1, keepdims=True) + 1e-06)
    scaled_grad = norm_gain * moe_grad
    projection = jnp.sum(scaled_grad * resid_in, axis=-1, keepdims=True)
    resid_grad = (
        out_grad[0].astype(jnp.float32)
        + inv_rms * scaled_grad
        - inv_rms * inv_rms * inv_rms / model_width * resid_in * projection
    )
    resid_grad = resid_grad.astype(jnp.bfloat16)[None]
    group_resid = lax.all_gather(resid_grad, "tensor", axis=1, tiled=True)
    group_rows = group_resid[0]
    attn_sum = lax.dot_general(
        group_rows,
        lax.all_gather(out_proj, "expert", axis=1, tiled=True),
        contract_last,
        preferred_element_type=jnp.float32,
    )
    attn_grad = attn_sum.astype(jnp.bfloat16)[None]
    return (resid_grad, attn_grad, down_grad)


MESH_ID = pl.DeviceIdType.MESH
ROUTE_LANES = 128
GATHER_ORDERS = (("z", "y", "x"), ("z", "x", "y"), ("x", "z", "y"), ("y", "z", "x"))
VMEM_SPEC = pl.BlockSpec(memory_space=pltpu.VMEM)


def place():
    expert = lax.axis_index("expert")
    return {
        "z": expert // 4,
        "y": lax.rem(expert // 2, 2),
        "c": lax.rem(expert, 2),
        "x": lax.axis_index("tensor"),
    }


def device_at(at):
    return {"expert": (at["z"] * 2 + at["y"]) * 2 + at["c"], "tensor": at["x"]}


def moved(at, axis, step, sizes):
    return {**at, axis: lax.rem(at[axis] + step, sizes[axis])}


def greet(at, sizes, axes):
    barrier = pltpu.get_barrier_semaphore()
    count = 0
    for axis in axes:
        for step in range(1, sizes[axis]):
            pl.semaphore_signal(
                barrier,
                inc=1,
                device_id=device_at(moved(at, axis, step, sizes)),
                device_id_type=MESH_ID,
            )
            count += 1
    pl.semaphore_wait(barrier, count)


def column_chunks(width, count):
    tiles = width // 128
    edges = [tiles * i // count * 128 for i in range(count + 1)]
    return [(edges[i], edges[i + 1] - edges[i]) for i in range(count)]


def gather_kernel(sizes, x_ref, out_ref, own_sem, send_sem, recv_sem):
    at = place()
    chunks = column_chunks(x_ref.shape[1], len(GATHER_ORDERS))
    own = pltpu.make_async_copy(
        x_ref, out_ref.at[at["z"], at["y"], at["c"], at["x"]], own_sem
    )
    own.start()
    greet(at, sizes, "zyxc")
    own.wait()

    def stage(chunk, number, axis, done):
        start, width = chunks[chunk]
        index = tuple(
            slice(None) if name in done else at[name] for name in "zycx"
        ) + (slice(None), pl.ds(start, width))
        copies = []
        for step in range(1, sizes[axis]):
            copy = pltpu.make_async_remote_copy(
                src_ref=out_ref.at[index],
                dst_ref=out_ref.at[index],
                send_sem=send_sem.at[chunk, number, step - 1],
                recv_sem=recv_sem.at[chunk, number, step - 1],
                device_id=device_at(moved(at, axis, step, sizes)),
                device_id_type=MESH_ID,
            )
            copy.start()
            copies.append(copy)
        return copies

    pending = {}
    everything = []
    for number in range(4):
        for chunk, order in enumerate(GATHER_ORDERS):
            full = order + ("c",)
            for copy in pending.get(chunk, ()):
                copy.wait_recv()
            pending[chunk] = stage(chunk, number, full[number], full[:number])
            everything += pending[chunk]
    for chunk in range(len(GATHER_ORDERS)):
        for copy in pending[chunk]:
            copy.wait_recv()
    for copy in everything:
        copy.wait_send()


def gather_all(rows, sizes):
    shape = (sizes["z"], sizes["y"], sizes["c"], sizes["x"]) + rows.shape
    most = max(sizes.values()) - 1
    count = len(GATHER_ORDERS)
    return pl.pallas_call(
        functools.partial(gather_kernel, sizes),
        out_shape=jax.ShapeDtypeStruct(shape, rows.dtype),
        in_specs=[VMEM_SPEC],
        out_specs=VMEM_SPEC,
        scratch_shapes=[
            pltpu.SemaphoreType.DMA,
            pltpu.SemaphoreType.DMA((count, 4, most)),
            pltpu.SemaphoreType.DMA((count, 4, most)),
        ],
        compiler_params=pltpu.CompilerParams(collective_id=0, has_side_effects=True),
    )(rows)


def added(first, second):
    return (first.astype(jnp.float32) + second.astype(jnp.float32)).astype(jnp.bfloat16)


def scatter_kernel(
    sizes,
    part_ref,
    out_grad_ref,
    norm_input_ref,
    norm_gain_ref,
    resid_ref,
    acc_ref,
    from_core,
    from_x,
    from_y,
    from_z,
    moe_ref,
    send_sem,
    recv_sem,
):
    at = place()
    width_all = part_ref.shape[-1]
    chunks = column_chunks(width_all, len(GATHER_ORDERS))
    landing = {"x": from_x, "y": from_y, "z": from_z}
    greet(at, sizes, "zyxc")
    everything = []

    def send(source, target, axis, step, chunk, number):
        copy = pltpu.make_async_remote_copy(
            src_ref=source,
            dst_ref=target,
            send_sem=send_sem.at[chunk, number, step - 1],
            recv_sem=recv_sem.at[chunk, number, step - 1],
            device_id=device_at(moved(at, axis, step, sizes)),
            device_id_type=MESH_ID,
        )
        copy.start()
        everything.append(copy)
        return copy

    pending = {}
    for chunk, (start, width) in enumerate(chunks):
        cols = pl.ds(start, width)
        pending[chunk] = [
            send(
                part_ref.at[:, :, 1 - at["c"], :, :, cols],
                from_core.at[:, :, :, :, cols],
                "c",
                1,
                chunk,
                0,
            )
        ]
    for number in range(1, 5):
        for chunk, (start, width) in enumerate(chunks):
            cols = pl.ds(start, width)
            order = GATHER_ORDERS[chunk][::-1]
            for copy in pending[chunk]:
                copy.wait_recv()
            if number == 1:
                for z in range(sizes["z"]):
                    acc_ref[z, :, :, :, cols] = added(
                        part_ref[z, :, at["c"], :, :, cols], from_core[z, :, :, :, cols]
                    )
            else:
                axis, left = order[number - 2], order[number - 1:]
                where = tuple(slice(None) if n in left else at[n] for n in "zyx")
                total = acc_ref[where + (slice(None), cols)].astype(jnp.float32)
                for step in range(1, sizes[axis]):
                    index = (step - 1,) + tuple(
                        slice(None) if n in left else 0 for n in "zyx"
                    )
                    total = total + landing[axis][index + (slice(None), cols)].astype(
                        jnp.float32
                    )
                if number == 4:
                    moe_ref[:, cols] = total
                else:
                    acc_ref[where + (slice(None), cols)] = total.astype(jnp.bfloat16)
            if number < 4:
                axis, left = order[number - 1], order[number:]
                pending[chunk] = []
                for step in range(1, sizes[axis]):
                    to = moved(at, axis, step, sizes)
                    source = tuple(slice(None) if n in left else to[n] for n in "zyx")
                    target = (step - 1,) + tuple(
                        slice(None) if n in left else 0 for n in "zyx"
                    )
                    pending[chunk].append(
                        send(
                            acc_ref.at[source + (slice(None), cols)],
                            landing[axis].at[target + (slice(None), cols)],
                            axis,
                            step,
                            chunk,
                            number,
                        )
                    )
    resid_in = norm_input_ref[...].astype(jnp.float32)
    inv_rms = lax.rsqrt(jnp.mean(resid_in * resid_in, axis=-1, keepdims=True) + 1e-06)
    scaled_grad = norm_gain_ref[...] * moe_ref[...]
    projection = jnp.sum(scaled_grad * resid_in, axis=-1, keepdims=True)
    resid_grad = (
        out_grad_ref[...].astype(jnp.float32)
        + inv_rms * scaled_grad
        - inv_rms * inv_rms * inv_rms / width_all * resid_in * projection
    )
    resid_ref[...] = resid_grad.astype(jnp.bfloat16)
    for copy in everything:
        copy.wait_send()


def scatter_and_norm(part, out_grad, norm_input, norm_gain, sizes):
    rows, width = out_grad.shape
    nz, ny, nx = sizes["z"], sizes["y"], sizes["x"]
    most = max(sizes.values()) - 1
    count = len(GATHER_ORDERS)
    bf16 = jnp.bfloat16
    return pl.pallas_call(
        functools.partial(scatter_kernel, sizes),
        out_shape=jax.ShapeDtypeStruct((rows, width), bf16),
        in_specs=[VMEM_SPEC] * 4,
        out_specs=VMEM_SPEC,
        scratch_shapes=[
            pltpu.VMEM((nz, ny, nx, rows, width), bf16),
            pltpu.VMEM((nz, ny, nx, rows, width), bf16),
            pltpu.VMEM((nx - 1, nz, ny, 1, rows, width), bf16),
            pltpu.VMEM((ny - 1, nz, 1, nx, rows, width), bf16),
            pltpu.VMEM((nz - 1, 1, ny, nx, rows, width), bf16),
            pltpu.VMEM((rows, width), jnp.float32),
            pltpu.SemaphoreType.DMA((count, 4, most)),
            pltpu.SemaphoreType.DMA((count, 4, most)),
        ],
        compiler_params=pltpu.CompilerParams(collective_id=1, has_side_effects=True),
    )(part, out_grad, norm_input, norm_gain)


def attn_kernel(
    sizes,
    resid_ref,
    proj_ref,
    attn_ref,
    cols_ref,
    part_ref,
    acc_ref,
    from_core,
    from_y,
    from_z,
    col_send,
    col_recv,
    send_sem,
    recv_sem,
):
    at = place()
    nz, ny, nc, nx = sizes["z"], sizes["y"], sizes["c"], sizes["x"]
    expert_count = nz * ny * nc
    total = expert_count * nx
    expert, half = lax.axis_index("expert"), at["x"]
    rows, share = cols_ref.shape[1], cols_ref.shape[2]
    me = expert * nx + half
    barrier = pltpu.get_barrier_semaphore()

    def other(step):
        number = lax.rem(me + step, total)
        return number // nx, lax.rem(number, nx)

    def signal(step, carry):
        to, to_half = other(step)
        pl.semaphore_signal(
            barrier,
            inc=1,
            device_id={"expert": to, "tensor": to_half},
            device_id_type=MESH_ID,
        )
        return carry

    lax.fori_loop(1, total, signal, 0)
    pl.semaphore_wait(barrier, total - 1)

    def column_copy(step):
        to, to_half = other(step)
        return pltpu.make_async_remote_copy(
            src_ref=resid_ref.at[:, pl.ds(pl.multiple_of(to * share, share), share)],
            dst_ref=cols_ref.at[me],
            send_sem=col_send.at[step],
            recv_sem=col_recv.at[step],
            device_id={"expert": to, "tensor": to_half},
            device_id_type=MESH_ID,
        )

    def start_columns(step, carry):
        column_copy(step).start()
        return carry

    def wait_columns(step, carry):
        column_copy(step).wait()
        return carry

    lax.fori_loop(1, total, start_columns, 0)
    own = pltpu.make_async_copy(
        resid_ref.at[:, pl.ds(pl.multiple_of(expert * share, share), share)],
        cols_ref.at[me],
        col_send.at[0],
    )
    own.start()
    own.wait()
    lax.fori_loop(1, total, wait_columns, 0)

    wanted = cols_ref[...].reshape(total * rows, share)
    chunks = column_chunks(proj_ref.shape[0], ATTN_CHUNKS)
    everything = []

    def send(source, target, axis, step, chunk, number):
        copy = pltpu.make_async_remote_copy(
            src_ref=source,
            dst_ref=target,
            send_sem=send_sem.at[chunk, number, step - 1],
            recv_sem=recv_sem.at[chunk, number, step - 1],
            device_id=device_at(moved(at, axis, step, sizes)),
            device_id_type=MESH_ID,
        )
        copy.start()
        everything.append(copy)
        return copy

    pending = {}
    for chunk, (start, width) in enumerate(chunks):
        cols = pl.ds(start, width)
        product = lax.dot_general(
            wanted,
            proj_ref[cols, :],
            (((1,), (1,)), ((), ())),
            preferred_element_type=jnp.float32,
        ).astype(jnp.bfloat16)
        part_ref[:, :, :, :, cols] = product.reshape(nz, ny, nc, nx * rows, width)
        pending[chunk] = [
            send(
                part_ref.at[:, :, 1 - at["c"], :, cols],
                from_core.at[:, :, :, cols],
                "c",
                1,
                chunk,
                0,
            )
        ]
    for chunk, (start, width) in enumerate(chunks):
        cols = pl.ds(start, width)
        pending[chunk][0].wait_recv()
        acc_ref[:, :, :, cols] = added(
            part_ref[:, :, at["c"], :, cols], from_core[:, :, :, cols]
        )
        pending[chunk] = [
            send(
                acc_ref.at[:, 1 - at["y"], :, cols],
                from_y.at[:, :, cols],
                "y",
                1,
                chunk,
                1,
            )
        ]
    for chunk, (start, width) in enumerate(chunks):
        cols = pl.ds(start, width)
        pending[chunk][0].wait_recv()
        acc_ref[:, at["y"], :, cols] = added(
            acc_ref[:, at["y"], :, cols], from_y[:, :, cols]
        )
        pending[chunk] = []
        for step in range(1, nz):
            to = moved(at, "z", step, sizes)
            pending[chunk].append(
                send(
                    acc_ref.at[to["z"], at["y"], :, cols],
                    from_z.at[step - 1, :, cols],
                    "z",
                    step,
                    chunk,
                    2,
                )
            )
    for chunk, (start, width) in enumerate(chunks):
        cols = pl.ds(start, width)
        sum_all = acc_ref[at["z"], at["y"], :, cols].astype(jnp.float32)
        for step in range(1, nz):
            pending[chunk][step - 1].wait_recv()
            sum_all = sum_all + from_z[step - 1, :, cols].astype(jnp.float32)
        attn_ref[:, cols] = sum_all.astype(jnp.bfloat16)
    for copy in everything:
        copy.wait_send()


ATTN_CHUNKS = 4


def attn_all(resid, proj, sizes):
    nz, ny, nc, nx = sizes["z"], sizes["y"], sizes["c"], sizes["x"]
    rows = resid.shape[0]
    width, share = proj.shape
    total = nz * ny * nc * nx
    most = max(sizes.values()) - 1
    bf16 = jnp.bfloat16
    return pl.pallas_call(
        functools.partial(attn_kernel, sizes),
        out_shape=jax.ShapeDtypeStruct((rows * nx, width), bf16),
        in_specs=[VMEM_SPEC] * 2,
        out_specs=VMEM_SPEC,
        scratch_shapes=[
            pltpu.VMEM((total, rows, share), bf16),
            pltpu.VMEM((nz, ny, nc, nx * rows, width), bf16),
            pltpu.VMEM((nz, ny, nx * rows, width), bf16),
            pltpu.VMEM((nz, ny, nx * rows, width), bf16),
            pltpu.VMEM((nz, nx * rows, width), bf16),
            pltpu.VMEM((nz - 1, nx * rows, width), bf16),
            pltpu.SemaphoreType.DMA((total,)),
            pltpu.SemaphoreType.DMA((total,)),
            pltpu.SemaphoreType.DMA((ATTN_CHUNKS, 3, most)),
            pltpu.SemaphoreType.DMA((ATTN_CHUNKS, 3, most)),
        ],
        compiler_params=pltpu.CompilerParams(collective_id=2, has_side_effects=True),
    )(resid, proj)


def split_three(values):
    high = lax.reduce_precision(values, 8, 7)
    middle = lax.reduce_precision(values - high, 8, 7)
    low = lax.reduce_precision(values - high - middle, 8, 7)
    return tuple(piece.astype(jnp.bfloat16) for piece in (high, middle, low))


def per_device_tokens(
    out_grad,
    norm_input,
    norm_gain,
    routes,
    route_weight,
    gate_saved,
    up_saved,
    w_gate,
    w_up,
    w_down,
    out_proj,
):
    expert_count = lax.axis_size("expert")
    expert = lax.axis_index("expert")
    slot_total = gate_saved.shape[1]
    slot_cap = slot_total // expert_count
    group_tokens = routes.shape[1]
    model_width = out_grad.shape[2]
    token_total = expert_count * group_tokens
    contract_last = (((1,), (1,)), ((), ()))
    contract_first = (((0,), (0,)), ((), ()))

    sizes = {"z": expert_count // 4, "y": 2, "c": 2, "x": lax.axis_size("tensor")}
    own_rows = out_grad.shape[1]
    first_row = lax.axis_index("tensor") * own_rows
    own_routes = lax.dynamic_slice_in_dim(routes[0], first_row, own_rows, 0)
    own_weight = lax.dynamic_slice_in_dim(route_weight[0], first_row, own_rows, 0)
    dense = jnp.sum(
        jnp.where(
            own_routes[:, :, None] == jnp.arange(expert_count, dtype=jnp.int32)[None, None, :],
            own_weight[:, :, None],
            0.0,
        ),
        axis=1,
    )
    pieces = split_three(dense)
    padding = jnp.zeros((own_rows, ROUTE_LANES - 3 * expert_count), jnp.bfloat16)
    rows = jnp.concatenate((out_grad[0],) + pieces + (padding,), axis=1)
    gathered = gather_all(rows, sizes).reshape(token_total, model_width + ROUTE_LANES)
    all_grads = gathered[:, :model_width]
    lane = jnp.arange(ROUTE_LANES, dtype=jnp.int32)
    mine = (lax.rem(lane, expert_count) == expert) & (lane < 3 * expert_count)
    weight = jnp.sum(
        jnp.where(mine[None, :], gathered[:, model_width:].astype(jnp.float32), 0.0), axis=-1
    ).reshape(expert_count, group_tokens)
    named = weight > 0.0
    before = jnp.tril(jnp.ones((group_tokens, group_tokens), jnp.float32), -1)
    rank = jnp.einsum("gt,ut->gu", named.astype(jnp.float32), before).astype(jnp.int32)
    slot = jnp.arange(expert_count, dtype=jnp.int32)[:, None] * slot_cap + rank
    slot = jnp.where(named, slot, -1).reshape(token_total, 1)
    pick = (slot == jnp.arange(slot_total, dtype=jnp.int32)[None, :]).astype(jnp.bfloat16)
    gate = lax.dot_general(
        pick, gate_saved[0], (((1,), (0,)), ((), ())), preferred_element_type=jnp.float32
    )
    upper = lax.dot_general(
        pick, up_saved[0], (((1,), (0,)), ((), ())), preferred_element_type=jnp.float32
    )
    sigmoid_gate = jax.nn.sigmoid(gate)
    activation = gate * sigmoid_gate
    hidden = (activation * upper).astype(jnp.bfloat16)

    token_grad = (weight.reshape(token_total, 1) * all_grads.astype(jnp.float32)).astype(
        jnp.bfloat16
    )
    hid_grad = lax.dot_general(
        token_grad, w_down[0], contract_last, preferred_element_type=jnp.float32
    )
    gate_grad = (hid_grad * upper * sigmoid_gate * (1.0 + gate * (1.0 - sigmoid_gate))).astype(
        jnp.bfloat16
    )
    up_grad = (hid_grad * activation).astype(jnp.bfloat16)
    part_grad = lax.dot_general(
        gate_grad, w_gate[0], contract_last, preferred_element_type=jnp.float32
    )
    part_grad = part_grad + lax.dot_general(
        up_grad, w_up[0], contract_last, preferred_element_type=jnp.float32
    )
    part_grad = part_grad.astype(jnp.bfloat16)
    down_grad = lax.dot_general(
        hidden, token_grad, contract_first, preferred_element_type=jnp.float32
    )
    down_grad = down_grad.astype(jnp.bfloat16)[None]
    part_grad = part_grad.reshape(
        sizes["z"], sizes["y"], sizes["c"], sizes["x"], own_rows, model_width
    )
    resid_grad = scatter_and_norm(
        part_grad, out_grad[0], norm_input[0], norm_gain[None], sizes
    )
    attn_grad = attn_all(resid_grad, out_proj, sizes)
    return (resid_grad[None], attn_grad[None], down_grad)


def per_device(*args):
    token_total = lax.axis_size("expert") * args[3].shape[1]
    if token_total <= args[5].shape[1]:
        return per_device_tokens(*args)
    return per_device_slots(*args)


def solution(mesh):
    placed = (
        P("expert", "tensor", None),
        P("expert", "tensor", None),
        P(),
        P("expert", None, None),
        P("expert", None, None),
        P("expert", None, "tensor"),
        P("expert", None, "tensor"),
        P("expert", None, "tensor"),
        P("expert", None, "tensor"),
        P("expert", "tensor", None),
        P("tensor", "expert"),
    )
    return jax.shard_map(
        per_device,
        mesh=mesh,
        in_specs=placed,
        out_specs=(
            P("expert", "tensor", None),
            P("expert", None, "tensor"),
            P("expert", "tensor", None),
        ),
        check_vma=False,
    )
```

```python
import functools
import jax
import jax.numpy as jnp
from jax import lax
from jax.experimental import pallas as pl
from jax.experimental.pallas import tpu as pltpu
from jax.sharding import PartitionSpec as P


def slot_position(route_ids, slot_cap, expert_count):
    flat_ids = route_ids.reshape(-1)
    one_hot = (flat_ids[:, None] == jnp.arange(expert_count, dtype=jnp.int32)[None, :]).astype(
        jnp.int32
    )
    earlier = jnp.cumsum(one_hot, axis=0) - one_hot
    slot_rank = jnp.sum(earlier * one_hot, axis=1)
    return flat_ids * slot_cap + slot_rank


def weighted_rows(token_rows, slot_token, slot_weight):
    picked_rows = token_rows[slot_token]
    return (slot_weight[:, None] * picked_rows.astype(jnp.float32)).astype(jnp.bfloat16)


def per_device_slots(
    out_grad,
    norm_input,
    norm_gain,
    routes,
    route_weight,
    gate_saved,
    up_saved,
    w_gate,
    w_up,
    w_down,
    out_proj,
):
    expert_count = lax.axis_size("expert")
    slot_cap = gate_saved.shape[1] // expert_count
    top_count = routes.shape[2]
    route_total = routes.shape[1] * top_count
    model_width = out_grad.shape[2]
    position = slot_position(routes[0], slot_cap, expert_count)
    source = (
        jnp.full((expert_count * slot_cap,), -1, jnp.int32)
        .at[position]
        .set(jnp.arange(route_total, dtype=jnp.int32))
    )
    filled = source >= 0
    safe_source = jnp.where(filled, source, 0)
    slot_weight = jnp.where(filled, route_weight[0].reshape(-1)[safe_source], jnp.float32(0.0))
    slot_token = safe_source // top_count
    group_grads = lax.all_gather(out_grad, "tensor", axis=1, tiled=True)
    scaled = weighted_rows(group_grads[0], slot_token, slot_weight)
    received = lax.all_to_all(
        scaled.reshape(expert_count, slot_cap, model_width),
        "expert",
        split_axis=0,
        concat_axis=0,
        tiled=True,
    )
    slot_grad = received.reshape(expert_count * slot_cap, model_width)
    contract_last = (((1,), (1,)), ((), ()))
    hid_grad = lax.dot_general(
        slot_grad, w_down[0], contract_last, preferred_element_type=jnp.float32
    )
    gate = gate_saved[0].astype(jnp.float32)
    upper = up_saved[0].astype(jnp.float32)
    sigmoid_gate = jax.nn.sigmoid(gate)
    activation = gate * sigmoid_gate
    gate_grad = (hid_grad * upper * sigmoid_gate * (1.0 + gate * (1.0 - sigmoid_gate))).astype(
        jnp.bfloat16
    )
    up_grad = (hid_grad * activation).astype(jnp.bfloat16)
    part_grad = lax.dot_general(
        gate_grad, w_gate[0], contract_last, preferred_element_type=jnp.float32
    )
    part_grad = part_grad + lax.dot_general(
        up_grad, w_up[0], contract_last, preferred_element_type=jnp.float32
    )
    part_grad = part_grad.astype(jnp.bfloat16)
    hidden = (activation * upper).astype(jnp.bfloat16)
    contract_first = (((0,), (0,)), ((), ()))
    block_sums = lax.psum_scatter(
        part_grad.astype(jnp.float32).astype(jnp.bfloat16),
        "tensor",
        scatter_dimension=1,
        tiled=True,
    ).astype(jnp.float32)
    feature_width = block_sums.shape[1]
    came_back = lax.all_to_all(
        block_sums.reshape(expert_count, slot_cap, feature_width).astype(jnp.bfloat16),
        "expert",
        split_axis=0,
        concat_axis=0,
        tiled=True,
    ).astype(jnp.float32)
    picked_part = came_back.reshape(expert_count * slot_cap, feature_width)[position]
    part_sum = jnp.sum(picked_part.reshape(-1, top_count, feature_width), axis=1)
    moe_grad = lax.all_to_all(
        part_sum.astype(jnp.bfloat16), "tensor", split_axis=0, concat_axis=1, tiled=True
    ).astype(part_sum.dtype)
    down_grad = lax.dot_general(
        hidden, slot_grad, contract_first, preferred_element_type=jnp.float32
    )
    down_grad = down_grad.astype(jnp.bfloat16)[None]
    resid_in = norm_input[0].astype(jnp.float32)
    inv_rms = lax.rsqrt(jnp.mean(resid_in * resid_in, axis=-1, keepdims=True) + 1e-06)
    scaled_grad = norm_gain * moe_grad
    projection = jnp.sum(scaled_grad * resid_in, axis=-1, keepdims=True)
    resid_grad = (
        out_grad[0].astype(jnp.float32)
        + inv_rms * scaled_grad
        - inv_rms * inv_rms * inv_rms / model_width * resid_in * projection
    )
    resid_grad = resid_grad.astype(jnp.bfloat16)[None]
    group_resid = lax.all_gather(resid_grad, "tensor", axis=1, tiled=True)
    group_rows = group_resid[0]
    attn_sum = lax.dot_general(
        group_rows,
        lax.all_gather(out_proj, "expert", axis=1, tiled=True),
        contract_last,
        preferred_element_type=jnp.float32,
    )
    attn_grad = attn_sum.astype(jnp.bfloat16)[None]
    return (resid_grad, attn_grad, down_grad)


MESH_ID = pl.DeviceIdType.MESH
ROUTE_LANES = 128
GATHER_ORDERS = (("z", "y", "x"), ("z", "x", "y"), ("x", "z", "y"), ("y", "z", "x")) * 2
CHUNK_SHARES = (5, 5, 3, 3) * 2
VMEM_SPEC = pl.BlockSpec(memory_space=pltpu.VMEM)


def place():
    expert = lax.axis_index("expert")
    return {
        "z": expert // 4,
        "y": lax.rem(expert // 2, 2),
        "c": lax.rem(expert, 2),
        "x": lax.axis_index("tensor"),
    }


def device_at(at):
    return {"expert": (at["z"] * 2 + at["y"]) * 2 + at["c"], "tensor": at["x"]}


def moved(at, axis, step, sizes):
    return {**at, axis: lax.rem(at[axis] + step, sizes[axis])}


def greet(at, sizes, axes):
    barrier = pltpu.get_barrier_semaphore()
    count = 0
    for axis in axes:
        for step in range(1, sizes[axis]):
            pl.semaphore_signal(
                barrier,
                inc=1,
                device_id=device_at(moved(at, axis, step, sizes)),
                device_id_type=MESH_ID,
            )
            count += 1
    pl.semaphore_wait(barrier, count)


def column_chunks(width, shares):
    tiles, whole = width // 128, sum(shares)
    edges = [tiles * sum(shares[:i]) // whole * 128 for i in range(len(shares) + 1)]
    return [(edges[i], edges[i + 1] - edges[i]) for i in range(len(shares))]


def finishing_order(sizes, orders, widths, gathers):
    free = {axis: 0.0 for axis in "zyxc"}
    events, done = [], []
    blocks = sizes["z"] * sizes["y"] * sizes["x"]

    def launch(now, chunk, stage, held):
        axis = orders[chunk][stage]
        count = sizes[axis]
        sent = held if gathers else held / count
        load = sent * widths[chunk] * {"z": 8.0, "y": 2.0, "x": 2.0, "c": 0.25}[axis]
        free[axis] = max(free[axis], now) + load
        left = held * count if gathers else held / count
        events.append((free[axis] + LATENCY, chunk, stage, left))

    for chunk in range(len(orders)):
        launch(0.0, chunk, 0, 1 if gathers else 2 * blocks)
    while events:
        event = min(events)
        events.remove(event)
        now, chunk, stage, held = event
        done.append((chunk, stage))
        if stage + 1 < len(orders[chunk]):
            launch(now, chunk, stage + 1, held)
    return done


LATENCY = 4000.0


def gather_kernel(sizes, x_ref, out_ref, own_sem, send_sem, recv_sem):
    at = place()
    chunks = column_chunks(x_ref.shape[1], CHUNK_SHARES)
    orders = [order + ("c",) for order in GATHER_ORDERS]
    own = pltpu.make_async_copy(
        x_ref, out_ref.at[at["z"], at["y"], at["c"], at["x"]], own_sem
    )
    own.start()
    greet(at, sizes, "zyxc")
    own.wait()

    def stage(chunk, number, axis, done):
        start, width = chunks[chunk]
        index = tuple(
            slice(None) if name in done else at[name] for name in "zycx"
        ) + (slice(None), pl.ds(start, width))
        copies = []
        for step in range(1, sizes[axis]):
            copy = pltpu.make_async_remote_copy(
                src_ref=out_ref.at[index],
                dst_ref=out_ref.at[index],
                send_sem=send_sem.at[chunk, number, step - 1],
                recv_sem=recv_sem.at[chunk, number, step - 1],
                device_id=device_at(moved(at, axis, step, sizes)),
                device_id_type=MESH_ID,
            )
            copy.start()
            copies.append(copy)
        return copies

    pending, everything = {}, []

    def begin(chunk, number):
        order = orders[chunk]
        pending[chunk] = stage(chunk, number, order[number], order[:number])
        everything.extend(pending[chunk])

    for chunk in range(len(chunks)):
        begin(chunk, 0)
    widths = [width for _, width in chunks]
    for chunk, number in finishing_order(sizes, orders, widths, True):
        for copy in pending[chunk]:
            copy.wait_recv()
        if number < 3:
            begin(chunk, number + 1)
    for copy in everything:
        copy.wait_send()


def gather_all(rows, sizes):
    shape = (sizes["z"], sizes["y"], sizes["c"], sizes["x"]) + rows.shape
    most = max(sizes.values()) - 1
    count = len(GATHER_ORDERS)
    return pl.pallas_call(
        functools.partial(gather_kernel, sizes),
        out_shape=jax.ShapeDtypeStruct(shape, rows.dtype),
        in_specs=[VMEM_SPEC],
        out_specs=VMEM_SPEC,
        scratch_shapes=[
            pltpu.SemaphoreType.DMA,
            pltpu.SemaphoreType.DMA((count, 4, most)),
            pltpu.SemaphoreType.DMA((count, 4, most)),
        ],
        compiler_params=pltpu.CompilerParams(collective_id=0, has_side_effects=True),
    )(rows)


def added(first, second):
    return (first.astype(jnp.float32) + second.astype(jnp.float32)).astype(jnp.bfloat16)


def scatter_kernel(
    sizes,
    part_ref,
    out_grad_ref,
    norm_input_ref,
    norm_gain_ref,
    resid_ref,
    acc_ref,
    from_core,
    from_x,
    from_y,
    from_z,
    moe_ref,
    send_sem,
    recv_sem,
):
    at = place()
    width_all = part_ref.shape[-1]
    chunks = column_chunks(width_all, CHUNK_SHARES)
    orders = [("c",) + order[::-1] for order in GATHER_ORDERS]
    landing = {"x": from_x, "y": from_y, "z": from_z}
    greet(at, sizes, "zyxc")
    everything = []

    def send(source, target, axis, step, chunk, number):
        copy = pltpu.make_async_remote_copy(
            src_ref=source,
            dst_ref=target,
            send_sem=send_sem.at[chunk, number, step - 1],
            recv_sem=recv_sem.at[chunk, number, step - 1],
            device_id=device_at(moved(at, axis, step, sizes)),
            device_id_type=MESH_ID,
        )
        copy.start()
        everything.append(copy)
        return copy

    pending = {}
    for chunk, (start, width) in enumerate(chunks):
        cols = pl.ds(start, width)
        pending[chunk] = [
            send(
                part_ref.at[:, :, 1 - at["c"], :, :, cols],
                from_core.at[:, :, :, :, cols],
                "c",
                1,
                chunk,
                0,
            )
        ]
    widths = [width for _, width in chunks]
    for chunk, ended in finishing_order(sizes, orders, widths, False):
        number = ended + 1
        cols = pl.ds(*chunks[chunk])
        order = orders[chunk][1:]
        for copy in pending[chunk]:
            copy.wait_recv()
        if number == 1:
            for z in range(sizes["z"]):
                acc_ref[z, :, :, :, cols] = added(
                    part_ref[z, :, at["c"], :, :, cols], from_core[z, :, :, :, cols]
                )
        else:
            axis, left = order[number - 2], order[number - 1:]
            where = tuple(slice(None) if n in left else at[n] for n in "zyx")
            total = acc_ref[where + (slice(None), cols)].astype(jnp.float32)
            for step in range(1, sizes[axis]):
                index = (step - 1,) + tuple(
                    slice(None) if n in left else 0 for n in "zyx"
                )
                total = total + landing[axis][index + (slice(None), cols)].astype(
                    jnp.float32
                )
            if number == 4:
                moe_ref[:, cols] = total
            else:
                acc_ref[where + (slice(None), cols)] = total.astype(jnp.bfloat16)
        if number < 4:
            axis, left = order[number - 1], order[number:]
            pending[chunk] = []
            for step in range(1, sizes[axis]):
                to = moved(at, axis, step, sizes)
                source = tuple(slice(None) if n in left else to[n] for n in "zyx")
                target = (step - 1,) + tuple(
                    slice(None) if n in left else 0 for n in "zyx"
                )
                pending[chunk].append(
                    send(
                        acc_ref.at[source + (slice(None), cols)],
                        landing[axis].at[target + (slice(None), cols)],
                        axis,
                        step,
                        chunk,
                        number,
                    )
                )
    resid_in = norm_input_ref[...].astype(jnp.float32)
    inv_rms = lax.rsqrt(jnp.mean(resid_in * resid_in, axis=-1, keepdims=True) + 1e-06)
    scaled_grad = norm_gain_ref[...] * moe_ref[...]
    projection = jnp.sum(scaled_grad * resid_in, axis=-1, keepdims=True)
    resid_grad = (
        out_grad_ref[...].astype(jnp.float32)
        + inv_rms * scaled_grad
        - inv_rms * inv_rms * inv_rms / width_all * resid_in * projection
    )
    resid_ref[...] = resid_grad.astype(jnp.bfloat16)
    for copy in everything:
        copy.wait_send()


def scatter_and_norm(part, out_grad, norm_input, norm_gain, sizes):
    rows, width = out_grad.shape
    nz, ny, nx = sizes["z"], sizes["y"], sizes["x"]
    most = max(sizes.values()) - 1
    count = len(GATHER_ORDERS)
    bf16 = jnp.bfloat16
    return pl.pallas_call(
        functools.partial(scatter_kernel, sizes),
        out_shape=jax.ShapeDtypeStruct((rows, width), bf16),
        in_specs=[VMEM_SPEC] * 4,
        out_specs=VMEM_SPEC,
        scratch_shapes=[
            pltpu.VMEM((nz, ny, nx, rows, width), bf16),
            pltpu.VMEM((nz, ny, nx, rows, width), bf16),
            pltpu.VMEM((nx - 1, nz, ny, 1, rows, width), bf16),
            pltpu.VMEM((ny - 1, nz, 1, nx, rows, width), bf16),
            pltpu.VMEM((nz - 1, 1, ny, nx, rows, width), bf16),
            pltpu.VMEM((rows, width), jnp.float32),
            pltpu.SemaphoreType.DMA((count, 4, most)),
            pltpu.SemaphoreType.DMA((count, 4, most)),
        ],
        compiler_params=pltpu.CompilerParams(collective_id=1, has_side_effects=True),
    )(part, out_grad, norm_input, norm_gain)


def attn_kernel(
    sizes,
    resid_ref,
    proj_ref,
    attn_ref,
    cols_ref,
    part_ref,
    acc_ref,
    from_core,
    from_y,
    from_z,
    col_send,
    col_recv,
    send_sem,
    recv_sem,
):
    at = place()
    nz, ny, nc, nx = sizes["z"], sizes["y"], sizes["c"], sizes["x"]
    expert_count = nz * ny * nc
    total = expert_count * nx
    expert, half = lax.axis_index("expert"), at["x"]
    rows, share = cols_ref.shape[1], cols_ref.shape[2]
    me = expert * nx + half
    barrier = pltpu.get_barrier_semaphore()

    def other(step):
        number = lax.rem(me + step, total)
        return number // nx, lax.rem(number, nx)

    def signal(step, carry):
        to, to_half = other(step)
        pl.semaphore_signal(
            barrier,
            inc=1,
            device_id={"expert": to, "tensor": to_half},
            device_id_type=MESH_ID,
        )
        return carry

    lax.fori_loop(1, total, signal, 0)
    pl.semaphore_wait(barrier, total - 1)

    def column_copy(step):
        to, to_half = other(step)
        return pltpu.make_async_remote_copy(
            src_ref=resid_ref.at[:, pl.ds(pl.multiple_of(to * share, share), share)],
            dst_ref=cols_ref.at[me],
            send_sem=col_send.at[step],
            recv_sem=col_recv.at[step],
            device_id={"expert": to, "tensor": to_half},
            device_id_type=MESH_ID,
        )

    def start_columns(step, carry):
        column_copy(step).start()
        return carry

    def wait_columns(step, carry):
        column_copy(step).wait()
        return carry

    lax.fori_loop(1, total, start_columns, 0)
    own = pltpu.make_async_copy(
        resid_ref.at[:, pl.ds(pl.multiple_of(expert * share, share), share)],
        cols_ref.at[me],
        col_send.at[0],
    )
    own.start()
    own.wait()
    lax.fori_loop(1, total, wait_columns, 0)

    wanted = cols_ref[...].reshape(total * rows, share)
    chunks = column_chunks(proj_ref.shape[0], (1,) * ATTN_CHUNKS)
    everything = []

    def send(source, target, axis, step, chunk, number):
        copy = pltpu.make_async_remote_copy(
            src_ref=source,
            dst_ref=target,
            send_sem=send_sem.at[chunk, number, step - 1],
            recv_sem=recv_sem.at[chunk, number, step - 1],
            device_id=device_at(moved(at, axis, step, sizes)),
            device_id_type=MESH_ID,
        )
        copy.start()
        everything.append(copy)
        return copy

    pending = {}
    for chunk, (start, width) in enumerate(chunks):
        cols = pl.ds(start, width)
        product = lax.dot_general(
            wanted,
            proj_ref[cols, :],
            (((1,), (1,)), ((), ())),
            preferred_element_type=jnp.float32,
        ).astype(jnp.bfloat16)
        part_ref[:, :, :, :, cols] = product.reshape(nz, ny, nc, nx * rows, width)
        pending[chunk] = [
            send(
                part_ref.at[:, :, 1 - at["c"], :, cols],
                from_core.at[:, :, :, cols],
                "c",
                1,
                chunk,
                0,
            )
        ]
    for chunk, (start, width) in enumerate(chunks):
        cols = pl.ds(start, width)
        pending[chunk][0].wait_recv()
        acc_ref[:, :, :, cols] = added(
            part_ref[:, :, at["c"], :, cols], from_core[:, :, :, cols]
        )
        pending[chunk] = [
            send(
                acc_ref.at[:, 1 - at["y"], :, cols],
                from_y.at[:, :, cols],
                "y",
                1,
                chunk,
                1,
            )
        ]
    for chunk, (start, width) in enumerate(chunks):
        cols = pl.ds(start, width)
        pending[chunk][0].wait_recv()
        acc_ref[:, at["y"], :, cols] = added(
            acc_ref[:, at["y"], :, cols], from_y[:, :, cols]
        )
        pending[chunk] = []
        for step in range(1, nz):
            to = moved(at, "z", step, sizes)
            pending[chunk].append(
                send(
                    acc_ref.at[to["z"], at["y"], :, cols],
                    from_z.at[step - 1, :, cols],
                    "z",
                    step,
                    chunk,
                    2,
                )
            )
    for chunk, (start, width) in enumerate(chunks):
        cols = pl.ds(start, width)
        sum_all = acc_ref[at["z"], at["y"], :, cols].astype(jnp.float32)
        for step in range(1, nz):
            pending[chunk][step - 1].wait_recv()
            sum_all = sum_all + from_z[step - 1, :, cols].astype(jnp.float32)
        attn_ref[:, cols] = sum_all.astype(jnp.bfloat16)
    for copy in everything:
        copy.wait_send()


ATTN_CHUNKS = 8


def attn_all(resid, proj, sizes):
    nz, ny, nc, nx = sizes["z"], sizes["y"], sizes["c"], sizes["x"]
    rows = resid.shape[0]
    width, share = proj.shape
    total = nz * ny * nc * nx
    most = max(sizes.values()) - 1
    bf16 = jnp.bfloat16
    return pl.pallas_call(
        functools.partial(attn_kernel, sizes),
        out_shape=jax.ShapeDtypeStruct((rows * nx, width), bf16),
        in_specs=[VMEM_SPEC] * 2,
        out_specs=VMEM_SPEC,
        scratch_shapes=[
            pltpu.VMEM((total, rows, share), bf16),
            pltpu.VMEM((nz, ny, nc, nx * rows, width), bf16),
            pltpu.VMEM((nz, ny, nx * rows, width), bf16),
            pltpu.VMEM((nz, ny, nx * rows, width), bf16),
            pltpu.VMEM((nz, nx * rows, width), bf16),
            pltpu.VMEM((nz - 1, nx * rows, width), bf16),
            pltpu.SemaphoreType.DMA((total,)),
            pltpu.SemaphoreType.DMA((total,)),
            pltpu.SemaphoreType.DMA((ATTN_CHUNKS, 3, most)),
            pltpu.SemaphoreType.DMA((ATTN_CHUNKS, 3, most)),
        ],
        compiler_params=pltpu.CompilerParams(collective_id=2, has_side_effects=True),
    )(resid, proj)


def split_three(values):
    high = lax.reduce_precision(values, 8, 7)
    middle = lax.reduce_precision(values - high, 8, 7)
    low = lax.reduce_precision(values - high - middle, 8, 7)
    return tuple(piece.astype(jnp.bfloat16) for piece in (high, middle, low))


def per_device_tokens(
    out_grad,
    norm_input,
    norm_gain,
    routes,
    route_weight,
    gate_saved,
    up_saved,
    w_gate,
    w_up,
    w_down,
    out_proj,
):
    expert_count = lax.axis_size("expert")
    expert = lax.axis_index("expert")
    slot_total = gate_saved.shape[1]
    slot_cap = slot_total // expert_count
    group_tokens = routes.shape[1]
    model_width = out_grad.shape[2]
    token_total = expert_count * group_tokens
    contract_last = (((1,), (1,)), ((), ()))
    contract_first = (((0,), (0,)), ((), ()))

    sizes = {"z": expert_count // 4, "y": 2, "c": 2, "x": lax.axis_size("tensor")}
    own_rows = out_grad.shape[1]
    first_row = lax.axis_index("tensor") * own_rows
    own_routes = lax.dynamic_slice_in_dim(routes[0], first_row, own_rows, 0)
    own_weight = lax.dynamic_slice_in_dim(route_weight[0], first_row, own_rows, 0)
    dense = jnp.sum(
        jnp.where(
            own_routes[:, :, None] == jnp.arange(expert_count, dtype=jnp.int32)[None, None, :],
            own_weight[:, :, None],
            0.0,
        ),
        axis=1,
    )
    pieces = split_three(dense)
    padding = jnp.zeros((own_rows, ROUTE_LANES - 3 * expert_count), jnp.bfloat16)
    rows = jnp.concatenate((out_grad[0],) + pieces + (padding,), axis=1)
    gathered = gather_all(rows, sizes).reshape(token_total, model_width + ROUTE_LANES)
    all_grads = gathered[:, :model_width]
    lane = jnp.arange(ROUTE_LANES, dtype=jnp.int32)
    mine = (lax.rem(lane, expert_count) == expert) & (lane < 3 * expert_count)
    weight = jnp.sum(
        jnp.where(mine[None, :], gathered[:, model_width:].astype(jnp.float32), 0.0), axis=-1
    ).reshape(expert_count, group_tokens)
    named = weight > 0.0
    before = jnp.tril(jnp.ones((group_tokens, group_tokens), jnp.float32), -1)
    rank = jnp.einsum("gt,ut->gu", named.astype(jnp.float32), before).astype(jnp.int32)
    slot = jnp.arange(expert_count, dtype=jnp.int32)[:, None] * slot_cap + rank
    slot = jnp.where(named, slot, -1).reshape(token_total, 1)
    pick = (slot == jnp.arange(slot_total, dtype=jnp.int32)[None, :]).astype(jnp.bfloat16)
    gate = lax.dot_general(
        pick, gate_saved[0], (((1,), (0,)), ((), ())), preferred_element_type=jnp.float32
    )
    upper = lax.dot_general(
        pick, up_saved[0], (((1,), (0,)), ((), ())), preferred_element_type=jnp.float32
    )
    sigmoid_gate = jax.nn.sigmoid(gate)
    activation = gate * sigmoid_gate
    hidden = (activation * upper).astype(jnp.bfloat16)

    token_grad = (weight.reshape(token_total, 1) * all_grads.astype(jnp.float32)).astype(
        jnp.bfloat16
    )
    hid_grad = lax.dot_general(
        token_grad, w_down[0], contract_last, preferred_element_type=jnp.float32
    )
    gate_grad = (hid_grad * upper * sigmoid_gate * (1.0 + gate * (1.0 - sigmoid_gate))).astype(
        jnp.bfloat16
    )
    up_grad = (hid_grad * activation).astype(jnp.bfloat16)
    part_grad = lax.dot_general(
        gate_grad, w_gate[0], contract_last, preferred_element_type=jnp.float32
    )
    part_grad = part_grad + lax.dot_general(
        up_grad, w_up[0], contract_last, preferred_element_type=jnp.float32
    )
    part_grad = part_grad.astype(jnp.bfloat16)
    down_grad = lax.dot_general(
        hidden, token_grad, contract_first, preferred_element_type=jnp.float32
    )
    down_grad = down_grad.astype(jnp.bfloat16)[None]
    part_grad = part_grad.reshape(
        sizes["z"], sizes["y"], sizes["c"], sizes["x"], own_rows, model_width
    )
    resid_grad = scatter_and_norm(
        part_grad, out_grad[0], norm_input[0], norm_gain[None], sizes
    )
    attn_grad = attn_all(resid_grad, out_proj, sizes)
    return (resid_grad[None], attn_grad[None], down_grad)


def per_device(*args):
    token_total = lax.axis_size("expert") * args[3].shape[1]
    if token_total <= args[5].shape[1]:
        return per_device_tokens(*args)
    return per_device_slots(*args)


def solution(mesh):
    placed = (
        P("expert", "tensor", None),
        P("expert", "tensor", None),
        P(),
        P("expert", None, None),
        P("expert", None, None),
        P("expert", None, "tensor"),
        P("expert", None, "tensor"),
        P("expert", None, "tensor"),
        P("expert", None, "tensor"),
        P("expert", "tensor", None),
        P("tensor", "expert"),
    )
    return jax.shard_map(
        per_device,
        mesh=mesh,
        in_specs=placed,
        out_specs=(
            P("expert", "tensor", None),
            P("expert", None, "tensor"),
            P("expert", "tensor", None),
        ),
        check_vma=False,
    )
```
